256 devices in a mesh: cuts: 8 (over y, z_lo), ctx: 32 (over z_hi, x, core).
Axes of the slice: x: 4, y: 4, z: 8 (z_hi: 4, z_lo: 2; z = z_hi * 2 + z_lo), core: 2. Of those that a mesh axis runs over, the one named last changes fastest.
Arguments:
- queries: bfloat16 [8192, 8192], P('ctx')
- keys: bfloat16 [8192, 1024], P(('cuts', 'ctx'))
- values: bfloat16 [8192, 1024], P(('cuts', 'ctx')), may hold values from -6 to 6
- bounds: int32 [3, 64], replicated, may hold values from 0 to 63, as said below
Outputs:
- attended: bfloat16 [8192, 8192], P('ctx', 'cuts')
The draws below stay inside these ranges and needn't reach their ends.
Inputs may be any that keep to these rules, and one draw needn't show every extreme that they name: The sequence is a row of trees laid end to end in whole mask blocks: each tree is a prompt of 1 to 4 mask blocks followed by up to 8 responses of 1 to 2 mask blocks each, so a tree spans at most 20 mask blocks; the last mask block is a one-block prompt of its own, and the tree before it may be cut off. For a block b of a prompt, bounds[0, b] is the prompt's first block and bounds[1, b] = bounds[2, b] = bounds[0, b]; for a block of a response, bounds[0, b] is the response's first block and bounds[1, b] < bounds[2, b] <= bounds[0, b] delimit the prompt of its tree. Block 0 starts a prompt.
All inputs are finite; a program needn't handle non-finite values.
Results may differ from the reference program's by a relative error of at most 0.014.
Values may be sent and summed in bfloat16 or wider, within the bound.
A program may use at most 64 MiB of HBM per device.

```python
import jax
import jax.numpy as jnp
from jax import lax

QUERY_HEADS = 64
KEY_VALUE_HEADS = 8
HEAD_SIZE = 128
BLK = 128
BRANCH = 8
QUERY_TOKENS = 256
PACKED_TOKENS = 8192
NB = 64
GROUP_SIZE = 8
N_CUTS = 8
N_CTX = 32


def key_base(key):
    base_offset = jax.random.normal(jax.random.fold_in(key, 21), (PACKED_TOKENS, KEY_VALUE_HEADS * HEAD_SIZE), jnp.float32)
    return base_offset


def draw_keys(key, part):
    return key_base(key).astype(jnp.bfloat16)


def draw_queries(key, part):
    drawn = jax.random.normal(jax.random.fold_in(key, 22), (PACKED_TOKENS, QUERY_HEADS * HEAD_SIZE), jnp.float32)
    return drawn.astype(jnp.bfloat16)


def draw_bounds(key, part):
    trees = NB
    segments = trees * (BRANCH + 1)
    prompt_key = jax.random.fold_in(key, 31)
    reply_key = jax.random.fold_in(key, 32)
    prompt_blocks = jax.random.randint(prompt_key, (trees, 1), 1, 5, dtype=jnp.int32)
    reply_blocks = jax.random.randint(reply_key, (trees, BRANCH), 1, 3, dtype=jnp.int32)
    lengths = jnp.concatenate([prompt_blocks, reply_blocks], axis=1).reshape(segments)
    segment_ends = jnp.cumsum(lengths).astype(jnp.int32)
    segment_starts = segment_ends - lengths
    blocks = jnp.arange(NB, dtype=jnp.int32)
    which_segment = jnp.sum((segment_starts[None, :] <= blocks[:, None]).astype(jnp.int32), axis=1) - 1
    labels = jnp.arange(segments, dtype=jnp.int32)
    select_own = (which_segment[:, None] == labels[None, :]).astype(jnp.int32)
    own_start = jnp.sum(select_own * segment_starts[None, :], axis=1)
    root_segment = which_segment // (BRANCH + 1) * (BRANCH + 1)
    select_root = (root_segment[:, None] == labels[None, :]).astype(jnp.int32)
    prompt_start = jnp.sum(select_root * segment_starts[None, :], axis=1)
    prompt_end = jnp.sum(select_root * segment_ends[None, :], axis=1)
    is_prompt = which_segment == root_segment
    prompt_end = jnp.where(is_prompt, prompt_start, prompt_end)
    is_last = blocks == NB - 1
    own_start = jnp.where(is_last, NB - 1, own_start)
    prompt_start = jnp.where(is_last, NB - 1, prompt_start)
    prompt_end = jnp.where(is_last, NB - 1, prompt_end)
    return jnp.stack([own_start, prompt_start, prompt_end], axis=0).astype(jnp.int32)


def block_levels(key, dims, pieces, smallest, high):
    factor_of = 1.0
    for position, parts in pieces:
        heights = jax.random.uniform(jax.random.fold_in(jax.random.fold_in(key, 6), position), (parts,), jnp.float32, smallest / len(pieces), high / len(pieces))
        factor_of = factor_of * jnp.repeat(jnp.exp(heights), dims[position] // parts).reshape((-1,) + (1,) * (len(dims) - 1 - position))
    return factor_of


def normal_values(key, dims, width, limit, shards=(), kind=jnp.bfloat16):
    gain = block_levels(key, dims, shards, -0.22, 0.18) if shards else 1.0
    entries = jax.random.normal(key, dims, jnp.float32) * width * gain
    return jnp.minimum(jnp.maximum(entries, -limit), limit).astype(kind)


def setup_inputs(seed: int = 0) -> dict:
    splits = jax.random.split(jax.random.key(seed), 5)
    queries = draw_queries(jax.random.fold_in(splits[4], 71), 0)
    keys = draw_keys(jax.random.fold_in(splits[4], 71), 0)
    values = normal_values(splits[2], (PACKED_TOKENS, KEY_VALUE_HEADS * HEAD_SIZE), 1.0, 6.0, ((0, 256),))
    bounds = draw_bounds(jax.random.fold_in(splits[4], 71), 0)
    return {"queries": queries, "keys": keys, "values": values, "bounds": bounds}


NEGATIVE_FILL = -1e30


def visible(query_pos, key_pos, bounds):
    blocks = bounds.shape[1]
    query_block = query_pos // BLK
    select = (query_block[:, None] == jnp.arange(blocks, dtype=jnp.int32)[None, :]).astype(jnp.int32)
    table = jnp.sum(select[:, None, :] * bounds[None, :, :], axis=2)
    key_block = key_pos // BLK
    own_part = key_block[None, :] >= table[:, 0:1]
    prefix = (key_block[None, :] >= table[:, 1:2]) & (key_block[None, :] < table[:, 2:3])
    return (key_pos[None, :] <= query_pos[:, None]) & (own_part | prefix)


def reference(queries, keys, values, bounds):
    span_length = PACKED_TOKENS // N_CUTS
    query_matrix = queries.reshape(N_CTX, QUERY_TOKENS, KEY_VALUE_HEADS, GROUP_SIZE, HEAD_SIZE)
    key_matrix = keys.reshape(N_CUTS, span_length, KEY_VALUE_HEADS, HEAD_SIZE)
    value_matrix = values.reshape(N_CUTS, span_length, KEY_VALUE_HEADS, HEAD_SIZE)
    key_pos_all = jnp.arange(PACKED_TOKENS, dtype=jnp.int32).reshape(N_CUTS, span_length)

    def one_block(entry):
        query_block, block_id = entry
        query_pos = block_id * QUERY_TOKENS + jnp.arange(QUERY_TOKENS, dtype=jnp.int32)
        query_wide = query_block.astype(jnp.float32)
        score_list = []
        allow_list = []
        for which in range(N_CUTS):
            allowed = visible(query_pos, key_pos_all[which], bounds)
            raw_score = jnp.einsum("qhgd,khd->qhgk", query_wide, key_matrix[which].astype(jnp.float32)) * (HEAD_SIZE ** -0.5)
            score_list.append(jnp.where(allowed[:, None, None, :], raw_score, NEGATIVE_FILL))
            allow_list.append(allowed)
        highest = jnp.max(score_list[0], axis=3)
        for which in range(1, N_CUTS):
            highest = jnp.maximum(highest, jnp.max(score_list[which], axis=3))
        summed_weights = jnp.zeros((QUERY_TOKENS, KEY_VALUE_HEADS, GROUP_SIZE, HEAD_SIZE), jnp.float32)
        row_totals = jnp.zeros((QUERY_TOKENS, KEY_VALUE_HEADS, GROUP_SIZE), jnp.float32)
        for which in range(N_CUTS):
            expos = jnp.where(allow_list[which][:, None, None, :], jnp.exp(score_list[which] - highest[..., None]), 0.0)
            weight = expos.astype(jnp.bfloat16)
            partial_out = jnp.einsum("qhgk,khd->qhgd", weight.astype(jnp.float32), value_matrix[which].astype(jnp.float32))
            rounded = lax.optimization_barrier(partial_out.astype(jnp.bfloat16))
            summed_weights = summed_weights + rounded.astype(jnp.float32)
            row_totals = row_totals + jnp.sum(expos, axis=3)
        result = (summed_weights / row_totals[..., None]).astype(jnp.bfloat16)
        return result.reshape(QUERY_TOKENS, QUERY_HEADS * HEAD_SIZE)

    outputs = lax.map(one_block, (query_matrix, jnp.arange(N_CTX, dtype=jnp.int32)))
    return outputs.reshape(PACKED_TOKENS, QUERY_HEADS * HEAD_SIZE)
```

```python
import jax
import jax.numpy as jnp
from jax import lax
from jax.experimental import pallas as pl
from jax.experimental.pallas import tpu as pltpu
from jax.sharding import PartitionSpec as P

D = 128
QT = 32
G = 8
BLK = 128
NEG = -1e30
MESH = pl.DeviceIdType.MESH
SCALE = 128 ** -0.5 * 1.4426950408889634


def kernel(bounds, q_hbm, k_hbm, v_hbm, out_ref,
           q_v, kin, vin, kbuf, vbuf, kst, vst, kpre, vpre, kown, vown,
           in_sem, s1, r1, sa, ra, sb, rb, sp, rp):
    c = lax.axis_index("cuts")
    t = lax.axis_index("ctx")
    y, zl = c // 2, c % 2
    zh, x, core = t // 8, (t // 2) % 4, t % 2
    e = x // 2
    qr = (x % 2) * 2 + core

    q_copy = pltpu.make_async_copy(
        q_hbm.at[:, pl.ds(pl.multiple_of(c * (G * D), G * D), G * D)], q_v, in_sem.at[0])
    k_copy = pltpu.make_async_copy(k_hbm, kin, in_sem.at[1])
    v_copy = pltpu.make_async_copy(v_hbm, vin, in_sem.at[2])
    k_copy.start()
    v_copy.start()
    q_copy.start()

    extra = (zl == 1) & (zh >= 2)
    barrier = pltpu.get_barrier_semaphore()

    def ctx_of(row):
        return row * 8 + t % 8

    def greet_row(i, carry):
        yrel, zls, zhs = i // 8, (i // 4) % 2, i % 4
        ys = (zh + 3 + yrel) % 4
        cs, ts = ys * 2 + zls, ctx_of(zhs)

        @pl.when((cs != c) | (ts != t))
        def _():
            pl.semaphore_signal(barrier, inc=1, device_id=(cs, ts), device_id_type=MESH)

        return carry

    lax.fori_loop(0, 16, greet_row, 0)
    for zhs in (2, 3):
        cs, ts = ((zh + 2) % 4) * 2 + 1, ctx_of(zhs)

        @pl.when((cs != c) | (ts != t))
        def _():
            pl.semaphore_signal(barrier, inc=1, device_id=(cs, ts), device_id_type=MESH)

    for i in range(1, 8):
        xd, cd = (x + i // 2) % 4, (core + i % 2) % 2
        pl.semaphore_signal(barrier, inc=1, device_id=(c, zh * 8 + xd * 2 + cd),
                            device_id_type=MESH)

    self_own = (zh == y).astype(jnp.int32)
    self_prev = (zh == (y + 1) % 4).astype(jnp.int32)
    ex = extra.astype(jnp.int32)
    self_ex = (extra & (zh == (y + 2) % 4)).astype(jnp.int32)
    k_copy.wait()
    v_copy.wait()
    pl.semaphore_wait(barrier, 16 - self_own - self_prev + 8 * ex - self_ex + 7)

    slot1 = 2 + zl * 4 + zh

    def phase1(kv, src, dst, group, dc):
        ch = (c + dc) % 8
        row = (y + group) % 4
        slot = slot1 + 8 * (1 - group) if group < 2 else zh - 2
        piece = src.at[:, pl.ds(pl.multiple_of(ch * D, D), D)]
        ss = s1.at[kv, group * 8 + dc]
        remote = pltpu.make_async_remote_copy(
            src_ref=piece, dst_ref=dst.at[slot], send_sem=ss, recv_sem=r1.at[kv, slot],
            device_id=(ch, ctx_of(row)), device_id_type=MESH)
        here = pltpu.make_async_copy(piece, dst.at[slot], r1.at[kv, slot])
        return remote, here, row == zh

    def each_phase1(fn):
        for kv, src, dst in ((0, kin, kbuf), (1, vin, vbuf)):
            for group in (0, 1):
                for dc in range(8):
                    fn(kv, src, dst, group, dc)

            @pl.when(extra)
            def _():
                for dc in range(8):
                    fn(kv, src, dst, 2, dc)

    def start1(kv, src, dst, group, dc):
        remote, here, mine = phase1(kv, src, dst, group, dc)
        if dc:
            remote.start()
        else:
            @pl.when(mine)
            def _():
                here.start()

            @pl.when(jnp.logical_not(mine))
            def _():
                remote.start()

    def drain1(kv, src, dst, group, dc):
        remote, here, mine = phase1(kv, src, dst, group, dc)
        if dc:
            remote.wait_send()
        else:
            @pl.when(jnp.logical_not(mine))
            def _():
                remote.wait_send()

    each_phase1(start1)

    def target(i):
        xd, cd = (x + i // 2) % 4, (core + i % 2) % 2
        return xd, cd, (c, zh * 8 + xd * 2 + cd)

    def copies2(kv, i):
        buf, st, pre, own = ((kbuf, kst, kpre, kown), (vbuf, vst, vpre, vown))[kv]
        xd, cd, dev = target(i)
        s0 = 10 + 2 * xd + cd
        jobs = (
            (buf.at[s0], own.at[1 + e, qr], sa.at[kv, i], ra.at[kv, i]),
            (buf.at[s0 - 1], own.at[0, qr], sb.at[kv, i], rb.at[kv, i]),
            (st.at[i], pre.at[:, e, qr], sp.at[kv, i], rp.at[kv, i]),
        )
        made = []
        for src, dst, ss, rs in jobs:
            if i:
                made.append(pltpu.make_async_remote_copy(
                    src_ref=src, dst_ref=dst, send_sem=ss, recv_sem=rs,
                    device_id=dev, device_id_type=MESH))
            else:
                made.append(pltpu.make_async_copy(src, dst, rs))
        return made

    def phase2(kv):
        buf, st = ((kbuf, kst), (vbuf, vst))[kv]

        def arrived(s, carry):
            pltpu.make_async_copy(buf.at[s], buf.at[s], r1.at[kv, s]).wait()
            return carry

        lax.fori_loop(0, 18, arrived, 0)
        for i in range(8):
            xd, cd, _ = target(i)
            p = bounds[1, 16 * zh + 4 * xd + 2 * cd] - 16 * zh + 20
            first = jnp.clip((p - e + 1) // 2, 0, 16)
            for w in range(2):
                st[i, w] = buf[first + (first + w) % 2]
        for i in range(8):
            made = copies2(kv, i)
            made[0].start()

            @pl.when(e == 1)
            def _():
                made[1].start()

        for i in range(8):
            copies2(kv, i)[2].start()

    phase2(0)
    phase2(1)

    def finish(kv):
        st, pre, own = ((kst, kpre, kown), (vst, vpre, vown))[kv]
        for i in range(8):
            xs = (x + 4 - i // 2) % 4
            es = xs // 2
            pltpu.make_async_copy(own.at[0, 0], own.at[0, 0], ra.at[kv, i]).wait()

            @pl.when(es == 1)
            def _():
                pltpu.make_async_copy(own.at[0, 0], own.at[0, 0], rb.at[kv, i]).wait()

            pltpu.make_async_copy(st.at[0], st.at[0], rp.at[kv, i]).wait()

    finish(0)
    finish(1)
    q_copy.wait()

    b0 = 16 * zh + 4 * x + 2 * core
    p0 = bounds[1, b0]
    rows_i = lax.broadcasted_iota(jnp.int32, (2 * BLK, BLK), 0) % BLK
    cols_i = lax.broadcasted_iota(jnp.int32, (2 * BLK, BLK), 1)
    causal = cols_i <= rows_i
    kp = kpre[...].reshape(4 * BLK, D)
    vp = vpre[...].reshape(4 * BLK, D)
    ones = jnp.ones((6 * BLK, D), jnp.bfloat16)
    for i in range(2):
        b = b0 + i
        own0, lo, hi1 = bounds[0, b], bounds[1, b], bounds[2, b]
        response = lo < hi1
        hi = jnp.where(response, hi1, b)
        keep = []
        for u in range(4):
            block = p0 + (u + 64 - p0) % 4
            keep.append((lo <= block) & (block < hi))
        keep.append(response & (own0 < b))
        kc = jnp.concatenate([kp, kown[i:i + 2].reshape(2 * BLK, D)], axis=0)
        vc = jnp.concatenate([vp, vown[i:i + 2].reshape(2 * BLK, D)], axis=0)
        vc = jnp.concatenate([vc, ones], axis=1)
        for g in range(0, G, 2):
            q2 = jnp.concatenate(
                [q_v[i * BLK:(i + 1) * BLK, (g + h) * D:(g + h + 1) * D] for h in range(2)], axis=0)
            s = lax.dot_general(q2, kc, (((1,), (1,)), ((), ())),
                                preferred_element_type=jnp.float32) * SCALE
            tiles = []
            for u in range(6):
                tile = s[:, u * BLK:(u + 1) * BLK]
                tiles.append(jnp.where(keep[u] if u < 5 else causal, tile, NEG))
            top = tiles[0]
            for tile in tiles[1:]:
                top = jnp.maximum(top, tile)
            top = jnp.max(top, axis=1, keepdims=True)
            w = jnp.concatenate([jnp.exp2(tile - top).astype(jnp.bfloat16) for tile in tiles], axis=1)
            o = jnp.dot(w, vc, preferred_element_type=jnp.float32)
            o = (o[:, :D] / o[:, D:]).astype(jnp.bfloat16)
            for h in range(2):
                out_ref[i * BLK:(i + 1) * BLK, (g + h) * D:(g + h + 1) * D] = o[h * BLK:(h + 1) * BLK]

    each_phase1(drain1)
    for kv in range(2):
        for i in range(1, 8):
            made = copies2(kv, i)
            made[0].wait_send()

            @pl.when(e == 1)
            def _():
                made[1].wait_send()

            made[2].wait_send()


def local(queries, keys, values, bounds):
    dma = pltpu.SemaphoreType.DMA
    bf = jnp.bfloat16
    return pl.pallas_call(
        kernel,
        out_shape=jax.ShapeDtypeStruct((256, G * D), bf),
        in_specs=[pl.BlockSpec(memory_space=pltpu.SMEM)] + [pl.BlockSpec(memory_space=pl.ANY)] * 3,
        out_specs=pl.BlockSpec(memory_space=pltpu.VMEM),
        scratch_shapes=[
            pltpu.VMEM((256, G * D), bf),
            pltpu.VMEM((QT, G * D), bf), pltpu.VMEM((QT, G * D), bf),
            pltpu.VMEM((18, QT, D), bf), pltpu.VMEM((18, QT, D), bf),
            pltpu.VMEM((8, 2, QT, D), bf), pltpu.VMEM((8, 2, QT, D), bf),
            pltpu.VMEM((2, 2, 4, QT, D), bf), pltpu.VMEM((2, 2, 4, QT, D), bf),
            pltpu.VMEM((3, 4, QT, D), bf), pltpu.VMEM((3, 4, QT, D), bf),
            dma((3,)), dma((2, 24)), dma((2, 18)),
            dma((2, 8)), dma((2, 8)), dma((2, 8)), dma((2, 8)), dma((2, 8)), dma((2, 8)),
        ],
        compiler_params=pltpu.CompilerParams(collective_id=0, has_side_effects=True),
        cost_estimate=pl.CostEstimate(flops=8 * 10 ** 8, bytes_accessed=2 ** 21,
                                      transcendentals=1536 * 1024),
    )(bounds, queries, keys, values)


def solution(mesh):
    in_specs = (P("ctx", None), P(("cuts", "ctx"), None), P(("cuts", "ctx"), None), P())
    return jax.shard_map(local, mesh=mesh, in_specs=in_specs, out_specs=P("ctx", "cuts"),
                         check_vma=False)
```

```python
import jax
import jax.numpy as jnp
from jax import lax
from jax.experimental import pallas as pl
from jax.experimental.pallas import tpu as pltpu
from jax.sharding import PartitionSpec as P

D = 128
QT = 32
G = 8
BLK = 128
NEG = -1e30
MESH = pl.DeviceIdType.MESH
SCALE = 128 ** -0.5 * 1.4426950408889634


def kernel(bounds, q_hbm, k_hbm, v_hbm, out_hbm,
           q_v, kin, vin, ky, vy, kbuf, vbuf, kst, vst, kpre, vpre, kown, vown, w_v, out_v,
           gy, gz, gx, in_sem, out_sem, s1, r1, s2, r2, sa, ra, sb, rb, sp, rp):
    c = lax.axis_index("cuts")
    t = lax.axis_index("ctx")
    y, zl = c // 2, c % 2
    zh, x, core = t // 8, (t // 2) % 4, t % 2
    e = x // 2
    qr = (x % 2) * 2 + core

    k_copy = pltpu.make_async_copy(k_hbm, kin, in_sem.at[1])
    v_copy = pltpu.make_async_copy(v_hbm, vin, in_sem.at[2])
    q_copy = pltpu.make_async_copy(
        q_hbm.at[:, pl.ds(pl.multiple_of(c * (G * D), G * D), G * D)], q_v, in_sem.at[0])
    k_copy.start()
    v_copy.start()

    z = zh * 2 + zl
    xc = x * 2 + core
    device = (
        lambda p: (p * 2 + zl, t),
        lambda p: (y * 2 + p % 2, p // 2 * 8 + t % 8),
        lambda p: (c, zh * 8 + p),
    )
    lines = ((4, y), (8, z), (8, xc))
    greet = (gy, gz, gx)

    @pl.when(zh <= 1)
    def _():
        kbuf[0:10] = jnp.zeros((10, QT, D), jnp.bfloat16)
        vbuf[0:10] = jnp.zeros((10, QT, D), jnp.bfloat16)

    barrier = pltpu.get_barrier_semaphore()
    for line in range(3):
        size, me = lines[line]
        for p in range(1, size):
            @pl.when(me < p)
            def _():
                pl.semaphore_signal(barrier, inc=1, device_id=device[line](p), device_id_type=MESH)

    q_copy.start()
    behind = y + z + xc

    @pl.when(behind > 0)
    def _():
        pl.semaphore_wait(barrier, behind)

    for line in range(3):
        size, me = lines[line]
        for p in range(size - 1):
            @pl.when(p < me)
            def _():
                pl.semaphore_signal(greet[line].at[me], inc=1, device_id=device[line](p),
                                    device_id_type=MESH)

    def make(src, dst, ss, rs, dev, here):
        if here:
            return pltpu.make_async_copy(src, dst, rs)
        return pltpu.make_async_remote_copy(
            src_ref=src, dst_ref=dst, send_sem=ss, recv_sem=rs, device_id=dev, device_id_type=MESH)

    k_copy.wait()
    v_copy.wait()

    def copy_y(kv, i):
        src, dst = ((kin, ky), (vin, vy))[kv]
        yd = (y + i) % 4
        piece = src.at[:, pl.ds(pl.multiple_of(yd * (2 * D), 2 * D), 2 * D)]
        return make(piece, dst.at[y], s1.at[kv, i], r1.at[kv, y], device[0](yd), i == 0)

    extra = (zl == 1) & (zh >= 2)
    index = zl * 4 + zh

    def place_z(i):
        return (zh + i % 4) % 4, (zl + i // 4) % 2

    def copy_z(kv, i, group):
        src, dst = ((ky, kbuf), (vy, vbuf))[kv]
        row, head = place_z(i)
        piece = src.at[(row + 4 - group) % 4, :, pl.ds(pl.multiple_of(head * D, D), D)]
        slot = 10 - 8 * group + index if group < 2 else zh - 2
        return make(piece, dst.at[slot], s2.at[kv, i * 3 + group], r2.at[kv, slot],
                    device[1](row * 2 + head), i == 0)

    def groups_z(kv, i, fn):
        row = place_z(i)[0]
        fn(copy_z(kv, i, 0))

        @pl.when(row >= 1)
        def _():
            fn(copy_z(kv, i, 1))

        @pl.when((row >= 2) & extra)
        def _():
            fn(copy_z(kv, i, 2))

    def place_x(i):
        return (x + i // 2) % 4, (core + i % 2) % 2

    def copy_x(kv, i, which):
        buf, st, pre, own = ((kbuf, kst, kpre, kown), (vbuf, vst, vpre, vown))[kv]
        xd, cd = place_x(i)
        s0 = 10 + 2 * xd + cd
        src, dst, ss, rs = (
            (buf.at[s0], own.at[1 + e, qr], sa, ra),
            (buf.at[s0 - 1], own.at[0, qr], sb, rb),
            (st.at[i], pre.at[:, e, qr], sp, rp),
        )[which]
        return make(src, dst, ss.at[kv, i], rs.at[kv, i], device[2](xd * 2 + cd), i == 0)

    def meet(line, sender):
        size, me = lines[line]
        for p in range(1, size):
            @pl.when((p > me) & (p == sender))
            def _():
                pl.semaphore_wait(greet[line].at[p], 1)

    for i in (0, 1, 2, 3):
        if i:
            meet(0, (y + i) % 4)
        copy_y(0, i).start()
        copy_y(1, i).start()

    order_z = ((2, 6), (1, 5), (3, 7), (0, 4))
    for kv in range(2):
        buf = (ky, vy)[kv]
        seen = {v: set() for v in range(4)}
        for pair in order_z:
            need = {}
            for v in range(4):
                row = (v + pair[0]) % 4
                for yp in range(max(row - 2, 0), row + 1):
                    if yp not in seen[v]:
                        seen[v].add(yp)
                        need.setdefault(yp, []).append(v)
            for yp in sorted(need):
                hit = zh == need[yp][0]
                for v in need[yp][1:]:
                    hit = hit | (zh == v)

                @pl.when(hit)
                def _():
                    pltpu.make_async_copy(buf.at[0], buf.at[0], r1.at[kv, yp]).wait()

            for i in pair:
                if kv == 0 and i:
                    row, head = place_z(i)
                    meet(1, row * 2 + head)
                groups_z(kv, i, lambda copy: copy.start())

    for kv in range(2):
        buf, st = ((kbuf, kst), (vbuf, vst))[kv]

        def arrived(s, carry):
            pltpu.make_async_copy(buf.at[s], buf.at[s], r2.at[kv, s]).wait()
            return carry

        lax.fori_loop(jnp.where(zh == 0, 10, jnp.where(zh == 1, 2, 0)), 18, arrived, 0)
        for i in range(8):
            xd, cd = place_x(i)
            p = bounds[1, 16 * zh + 4 * xd + 2 * cd] - 16 * zh + 20
            first = jnp.clip((p - e + 1) // 2, 0, 16)
            for w in range(2):
                st[i, w] = buf[first + (first + w) % 2]
        for i in range(7, -1, -1):
            if kv == 0 and i:
                xd, cd = place_x(i)
                meet(2, xd * 2 + cd)
            copy_x(kv, i, 0).start()

            @pl.when(e == 1)
            def _():
                copy_x(kv, i, 1).start()

        for i in range(7, -1, -1):
            copy_x(kv, i, 2).start()

    def finish(kv):
        st, own = ((kst, kown), (vst, vown))[kv]
        for i in range(8):
            pltpu.make_async_copy(own.at[0, 0], own.at[0, 0], ra.at[kv, i]).wait()

            @pl.when((x + 4 - i // 2) % 4 >= 2)
            def _():
                pltpu.make_async_copy(own.at[0, 0], own.at[0, 0], rb.at[kv, i]).wait()

            pltpu.make_async_copy(st.at[0], st.at[0], rp.at[kv, i]).wait()

    b0 = 16 * zh + 4 * x + 2 * core
    p0 = bounds[1, b0]
    rows_i = lax.broadcasted_iota(jnp.int32, (2 * BLK, BLK), 0) % BLK
    cols_i = lax.broadcasted_iota(jnp.int32, (2 * BLK, BLK), 1)
    causal = cols_i <= rows_i
    q_copy.wait()
    finish(0)
    kp = kpre[...].reshape(4 * BLK, D)
    for i in range(2):
        b = b0 + i
        own0, lo, hi1 = bounds[0, b], bounds[1, b], bounds[2, b]
        response = lo < hi1
        hi = jnp.where(response, hi1, b)
        keep = []
        for u in range(4):
            block = p0 + (u + 64 - p0) % 4
            keep.append((lo <= block) & (block < hi))
        keep.append(response & (own0 < b))
        kc = jnp.concatenate([kp, kown[i:i + 2].reshape(2 * BLK, D)], axis=0)
        for g in range(0, G, 2):
            q2 = jnp.concatenate(
                [q_v[i * BLK:(i + 1) * BLK, (g + h) * D:(g + h + 1) * D] for h in range(2)], axis=0)
            s = lax.dot_general(q2, kc, (((1,), (1,)), ((), ())),
                                preferred_element_type=jnp.float32) * SCALE
            tiles = []
            for u in range(6):
                tile = s[:, u * BLK:(u + 1) * BLK]
                tiles.append(jnp.where(keep[u] if u < 5 else causal, tile, NEG))
            top = tiles[0]
            for tile in tiles[1:]:
                top = jnp.maximum(top, tile)
            top = jnp.max(top, axis=1, keepdims=True)
            for u in range(6):
                w_v[i * 4 + g // 2, :, u * BLK:(u + 1) * BLK] = jnp.exp2(tiles[u] - top).astype(jnp.bfloat16)

    finish(1)
    vp = vpre[...].reshape(4 * BLK, D)
    ones = jnp.ones((6 * BLK, D), jnp.bfloat16)

    def out_copy(i, g):
        part = (pl.ds(i * BLK, BLK), pl.ds(g * D, 2 * D))
        return pltpu.make_async_copy(out_v.at[part], out_hbm.at[part], out_sem.at[i * 4 + g // 2])

    for i in range(2):
        vc = jnp.concatenate([vp, vown[i:i + 2].reshape(2 * BLK, D)], axis=0)
        vc = jnp.concatenate([vc, ones], axis=1)
        for g in range(0, G, 2):
            o = jnp.dot(w_v[i * 4 + g // 2], vc, preferred_element_type=jnp.float32)
            o = (o[:, :D] / o[:, D:]).astype(jnp.bfloat16)
            for h in range(2):
                out_v[i * BLK:(i + 1) * BLK, (g + h) * D:(g + h + 1) * D] = o[h * BLK:(h + 1) * BLK]
            out_copy(i, g).start()

    for kv in range(2):
        for i in range(1, 4):
            copy_y(kv, i).wait_send()
        for i in range(1, 8):
            groups_z(kv, i, lambda copy: copy.wait_send())
            copy_x(kv, i, 0).wait_send()

            @pl.when(e == 1)
            def _():
                copy_x(kv, i, 1).wait_send()

            copy_x(kv, i, 2).wait_send()
    for i in range(2):
        for g in range(0, G, 2):
            out_copy(i, g).wait()


def local(queries, keys, values, bounds):
    dma = pltpu.SemaphoreType.DMA
    bf = jnp.bfloat16
    two = lambda *shape: [pltpu.VMEM(shape, bf)] * 2
    return pl.pallas_call(
        kernel,
        out_shape=jax.ShapeDtypeStruct((256, G * D), bf),
        in_specs=[pl.BlockSpec(memory_space=pltpu.SMEM)] + [pl.BlockSpec(memory_space=pl.ANY)] * 3,
        out_specs=pl.BlockSpec(memory_space=pl.ANY),
        scratch_shapes=[
            pltpu.VMEM((256, G * D), bf), *two(QT, G * D), *two(4, QT, 2 * D), *two(18, QT, D),
            *two(8, 2, QT, D), *two(2, 2, 4, QT, D), *two(3, 4, QT, D),
            pltpu.VMEM((8, 2 * BLK, 6 * BLK), bf), pltpu.VMEM((256, G * D), bf),
            *[pltpu.SemaphoreType.REGULAR((8,))] * 3,
            dma((3,)), dma((8,)), dma((2, 4)), dma((2, 4)), dma((2, 24)), dma((2, 18)),
            *[dma((2, 8))] * 6,
        ],
        compiler_params=pltpu.CompilerParams(collective_id=0, has_side_effects=True),
        cost_estimate=pl.CostEstimate(flops=8 * 10 ** 8, bytes_accessed=2 ** 21,
                                      transcendentals=1536 * 1024),
    )(bounds, queries, keys, values)


def solution(mesh):
    in_specs = (P("ctx", None), P(("cuts", "ctx"), None), P(("cuts", "ctx"), None), P())
    return jax.shard_map(local, mesh=mesh, in_specs=in_specs, out_specs=P("ctx", "cuts"),
                         check_vma=False)
```

```python
import jax
import jax.numpy as jnp
from jax import lax
from jax.experimental import pallas as pl
from jax.experimental.pallas import tpu as pltpu
from jax.sharding import PartitionSpec as P

D = 128
QT = 32
G = 8
BLK = 128
NEG = -1e30
MESH = pl.DeviceIdType.MESH
SCALE = 128 ** -0.5 * 1.4426950408889634


def rem(a, b):
    return lax.rem(a, jnp.int32(b))


def kernel(bounds, q_hbm, k_hbm, v_hbm, out_hbm,
           q_v, kvin, kvy, kbuf, vbuf, st, pre, own, w_v, out_v,
           gy, gz, gx, q_sem, in_sem, out_sem, sy, sz, sx, ry, rz, rx):
    c = lax.axis_index("cuts")
    t = lax.axis_index("ctx")
    y, zl = lax.div(c, jnp.int32(2)), rem(c, 2)
    zh, xc = lax.div(t, jnp.int32(8)), rem(t, 8)
    x, core = lax.div(xc, jnp.int32(2)), rem(xc, 2)
    e = lax.div(x, jnp.int32(2))
    qr = rem(x, 2) * 2 + core
    z = zh * 2 + zl

    both = (kbuf, vbuf)
    k_copy = pltpu.make_async_copy(k_hbm, kvin.at[0], in_sem)
    v_copy = pltpu.make_async_copy(v_hbm, kvin.at[1], in_sem)
    q_copy = pltpu.make_async_copy(
        q_hbm.at[:, pl.ds(pl.multiple_of(c * (G * D), G * D), G * D)], q_v, q_sem)
    k_copy.start()
    v_copy.start()

    device = (
        lambda p: (p * 2 + zl, t),
        lambda p: (y * 2 + p % 2, p // 2 * 8 + xc),
        lambda p: (c, zh * 8 + p),
    )
    lines = ((4, y, gy), (8, z, gz), (8, xc, gx))

    @pl.when(zh <= 1)
    def _():
        kbuf[0:10] = jnp.zeros((10, QT, D), jnp.bfloat16)
        vbuf[0:10] = jnp.zeros((10, QT, D), jnp.bfloat16)

    barrier = pltpu.get_barrier_semaphore()
    for line in range(3):
        size, me, _ = lines[line]
        for p in range(1, size):
            @pl.when(me < p)
            def _():
                pl.semaphore_signal(barrier, inc=1, device_id=device[line](p), device_id_type=MESH)

    q_copy.start()
    behind = y + z + xc

    @pl.when(behind > 0)
    def _():
        pl.semaphore_wait(barrier, behind)

    for line in range(3):
        size, me, sem = lines[line]
        for p in range(size - 1):
            @pl.when(p < me)
            def _():
                pl.semaphore_signal(sem, inc=1, device_id=device[line](p), device_id_type=MESH)

    def answered(line):
        size, me, sem = lines[line]

        @pl.when(me < size - 1)
        def _():
            pl.semaphore_wait(sem, size - 1 - me)

    def make(src, dst, ss, rs, dev, here):
        if here:
            return pltpu.make_async_copy(src, dst, rs)
        return pltpu.make_async_remote_copy(
            src_ref=src, dst_ref=dst, send_sem=ss, recv_sem=rs, device_id=dev, device_id_type=MESH)

    def wait_for(ref, sem):
        pltpu.make_async_copy(ref, ref, sem).wait()

    def copy_y(p, here):
        piece = kvin.at[:, :, pl.ds(pl.multiple_of(p * (2 * D), 2 * D), 2 * D)]
        return make(piece, kvy.at[:, y], sy, ry.at[y], device[0](p), here)

    extra = (zl == 1) & (zh >= 2)
    index = zl * 4 + zh
    first_row = jnp.where(zh >= 2, 0, zh + 1)

    def send_z(kv, k, h, group):
        row, head = rem(first_row + k, 4), zl if h == 0 else 1 - zl
        sent = row >= group
        if group == 2:
            sent = sent & extra

        def copy(here):
            piece = kvy.at[kv, row - group, :, pl.ds(pl.multiple_of(head * D, D), D)]
            slot = 10 - 8 * group + index if group < 2 else zh - 2
            return make(piece, both[kv].at[slot], sz.at[group], rz.at[kv, group],
                        (y * 2 + head, row * 8 + xc), here)

        if h:
            @pl.when(sent)
            def _():
                copy(False).start()
        else:
            @pl.when(sent & (row != zh))
            def _():
                copy(False).start()

            @pl.when(sent & (row == zh))
            def _():
                copy(True).start()

    def place_x(i):
        return rem(x + i // 2, 4), core if i % 2 == 0 else 1 - core

    def send_x(kv, i, which):
        xd, cd = place_x(i)
        s0 = 10 + 2 * xd + cd
        src, dst, rs = (
            (both[kv].at[s0], own.at[kv, 1 + e, qr], rx.at[kv, 0]),
            (both[kv].at[s0 - 1], own.at[kv, 0, qr], rx.at[kv, 0]),
            (st.at[kv, i], pre.at[kv, :, e, qr], rx.at[kv, 1]),
        )[which]
        make(src, dst, sx.at[which], rs, (c, zh * 8 + xd * 2 + cd), i == 0).start()

    wait_for(kvin, in_sem)
    for p in range(3):
        @pl.when(p < y)
        def _():
            copy_y(p, False).start()

    copy_y(y, True).start()
    answered(0)
    for p in range(1, 4):
        @pl.when(p > y)
        def _():
            copy_y(p, False).start()

    for kv in range(2):
        for k in range(4):
            if kv == 0:
                wait_for(kvy.at[:, 0], ry.at[rem(first_row + k, 4)])
                if k == 0:
                    answered(1)
            for h in range(2):
                send_z(kv, k, h, 0)
        for k in range(4):
            for h in range(2):
                send_z(kv, k, h, 1)
                send_z(kv, k, h, 2)

    answered(2)
    for kv in range(2):
        wait_for(both[kv].at[10:18], rz.at[kv, 0])

        @pl.when(zh >= 1)
        def _():
            wait_for(both[kv].at[2:10], rz.at[kv, 1])

        @pl.when(zh >= 2)
        def _():
            wait_for(both[kv].at[0:2], rz.at[kv, 2])

        for i in range(8):
            xd, cd = place_x(i)
            p = bounds[1, 16 * zh + 4 * xd + 2 * cd] - 16 * zh + 20
            first = jnp.clip(lax.shift_right_arithmetic(p - e + 1, 1), 0, 16)
            for w in range(2):
                st[kv, i, w] = both[kv][first + rem(first + w, 2)]
        for i in range(7, -1, -1):
            send_x(kv, i, 0)

        @pl.when(e == 1)
        def _():
            for i in range(7, -1, -1):
                send_x(kv, i, 1)

        for i in range(7, -1, -1):
            send_x(kv, i, 2)

    def arrived_x(kv):
        wait_for(own.at[kv], rx.at[kv, 0])
        wait_for(pre.at[kv], rx.at[kv, 1])

    b0 = 16 * zh + 4 * x + 2 * core
    p0 = bounds[1, b0]
    rows_i = lax.broadcasted_iota(jnp.int32, (2 * BLK, BLK), 0) % BLK
    cols_i = lax.broadcasted_iota(jnp.int32, (2 * BLK, BLK), 1)
    causal = cols_i <= rows_i
    q_copy.wait()
    arrived_x(0)
    kp = pre[0].reshape(4 * BLK, D)
    for i in range(2):
        b = b0 + i
        own0, lo, hi1 = bounds[0, b], bounds[1, b], bounds[2, b]
        response = lo < hi1
        hi = jnp.where(response, hi1, b)
        keep = []
        for u in range(4):
            block = p0 + (u + 64 - p0) % 4
            keep.append((lo <= block) & (block < hi))
        keep.append(response & (own0 < b))
        kc = jnp.concatenate([kp, own[0, i:i + 2].reshape(2 * BLK, D)], axis=0)
        for g in range(0, G, 2):
            q2 = jnp.concatenate(
                [q_v[i * BLK:(i + 1) * BLK, (g + h) * D:(g + h + 1) * D] for h in range(2)], axis=0)
            s = lax.dot_general(q2, kc, (((1,), (1,)), ((), ())),
                                preferred_element_type=jnp.float32) * SCALE
            tiles = []
            for u in range(6):
                tile = s[:, u * BLK:(u + 1) * BLK]
                tiles.append(jnp.where(keep[u] if u < 5 else causal, tile, NEG))
            top = tiles[0]
            for tile in tiles[1:]:
                top = jnp.maximum(top, tile)
            top = jnp.max(top, axis=1, keepdims=True)
            for u in range(6):
                w_v[i * 4 + g // 2, :, u * BLK:(u + 1) * BLK] = jnp.exp2(tiles[u] - top).astype(jnp.bfloat16)

    arrived_x(1)
    vp = pre[1].reshape(4 * BLK, D)
    ones = jnp.ones((6 * BLK, D), jnp.bfloat16)

    def out_copy(i, g):
        part = (pl.ds(i * BLK, BLK), pl.ds(g * D, 2 * D))
        return pltpu.make_async_copy(out_v.at[part], out_hbm.at[part], out_sem)

    for i in range(2):
        vc = jnp.concatenate([vp, own[1, i:i + 2].reshape(2 * BLK, D)], axis=0)
        vc = jnp.concatenate([vc, ones], axis=1)
        for g in range(0, G, 2):
            o = jnp.dot(w_v[i * 4 + g // 2], vc, preferred_element_type=jnp.float32)
            o = (o[:, :D] / o[:, D:]).astype(jnp.bfloat16)
            for h in range(2):
                out_v[i * BLK:(i + 1) * BLK, (g + h) * D:(g + h + 1) * D] = o[h * BLK:(h + 1) * BLK]
            out_copy(i, g).start()

    wait_for(kvy.at[:, 0:3], sy)
    wait_for(st.at[0, 0:7], sz.at[0])

    @pl.when(zh == 0)
    def _():
        wait_for(st.at[0, 0:6], sz.at[1])

    @pl.when(zh >= 1)
    def _():
        wait_for(st.at[0, 0:5], sz.at[1])

    @pl.when(extra)
    def _():
        wait_for(st.at[0, 0:3], sz.at[2])

    wait_for(st.at[0, 0:7], sx.at[0])

    @pl.when(e == 1)
    def _():
        wait_for(st.at[0, 0:7], sx.at[1])

    wait_for(st.at[:, 0:7], sx.at[2])
    pltpu.make_async_copy(out_v, out_hbm, out_sem).wait()


def local(queries, keys, values, bounds):
    dma = pltpu.SemaphoreType.DMA
    vmem = lambda *shape: pltpu.VMEM(shape, jnp.bfloat16)
    return pl.pallas_call(
        kernel,
        out_shape=jax.ShapeDtypeStruct((256, G * D), jnp.bfloat16),
        in_specs=[pl.BlockSpec(memory_space=pltpu.SMEM)] + [pl.BlockSpec(memory_space=pl.ANY)] * 3,
        out_specs=pl.BlockSpec(memory_space=pl.ANY),
        scratch_shapes=[
            vmem(256, G * D), vmem(2, QT, G * D), vmem(2, 4, QT, 2 * D), vmem(18, QT, D), vmem(18, QT, D),
            vmem(2, 8, 2, QT, D), vmem(2, 2, 2, 4, QT, D), vmem(2, 3, 4, QT, D),
            vmem(8, 2 * BLK, 6 * BLK), vmem(256, G * D),
            *[pltpu.SemaphoreType.REGULAR] * 3,
            dma, dma, dma, dma, dma((3,)), dma((3,)), dma((4,)), dma((2, 3)), dma((2, 2)),
        ],
        compiler_params=pltpu.CompilerParams(collective_id=0, has_side_effects=True),
        cost_estimate=pl.CostEstimate(flops=8 * 10 ** 8, bytes_accessed=2 ** 21,
                                      transcendentals=1536 * 1024),
    )(bounds, queries, keys, values)


def solution(mesh):
    in_specs = (P("ctx", None), P(("cuts", "ctx"), None), P(("cuts", "ctx"), None), P())
    return jax.shard_map(local, mesh=mesh, in_specs=in_specs, out_specs=P("ctx", "cuts"),
                         check_vma=False)
```

```python
import jax
import jax.numpy as jnp
from jax import lax
from jax.experimental import pallas as pl
from jax.experimental.pallas import tpu as pltpu
from jax.sharding import PartitionSpec as P

D = 128
QT = 32
G = 8
BLK = 128
NEG = -1e30
MESH = pl.DeviceIdType.MESH
SCALE = 128 ** -0.5 * 1.4426950408889634


def rem(a, b):
    return lax.rem(a, jnp.int32(b))


def kernel(bounds_hbm, q_hbm, k_hbm, v_hbm, out_ref,
           bounds, q_v, kvin, kvy, kbuf, vbuf, st, pre, own, w_v,
           gy, gz, gx, bounds_sem, q_sem, in_sem, sy, sz, sx, ry, rz, rx):
    c = lax.axis_index("cuts")
    t = lax.axis_index("ctx")
    y, zl = lax.div(c, jnp.int32(2)), rem(c, 2)
    zh, xc = lax.div(t, jnp.int32(8)), rem(t, 8)
    x, core = lax.div(xc, jnp.int32(2)), rem(xc, 2)
    e = lax.div(x, jnp.int32(2))
    qr = rem(x, 2) * 2 + core
    z = zh * 2 + zl

    both = (kbuf, vbuf)
    k_copy = pltpu.make_async_copy(k_hbm, kvin.at[0], in_sem)
    v_copy = pltpu.make_async_copy(v_hbm, kvin.at[1], in_sem)
    q_copy = pltpu.make_async_copy(
        q_hbm.at[:, pl.ds(pl.multiple_of(c * (G * D), G * D), G * D)], q_v, q_sem)
    k_copy.start()
    v_copy.start()
    bounds_copy = pltpu.make_async_copy(bounds_hbm, bounds, bounds_sem)
    bounds_copy.start()

    device = (
        lambda p: (p * 2 + zl, t),
        lambda p: (y * 2 + p % 2, p // 2 * 8 + xc),
        lambda p: (c, zh * 8 + p),
    )
    lines = ((4, y, gy), (8, z, gz), (8, xc, gx))

    @pl.when(zh <= 1)
    def _():
        kbuf[0:10] = jnp.zeros((10, QT, D), jnp.bfloat16)
        vbuf[0:10] = jnp.zeros((10, QT, D), jnp.bfloat16)

    barrier = pltpu.get_barrier_semaphore()
    for line in range(3):
        size, me, _ = lines[line]
        for p in range(1, size):
            @pl.when(me < p)
            def _():
                pl.semaphore_signal(barrier, inc=1, device_id=device[line](p), device_id_type=MESH)

    q_copy.start()
    behind = y + z + xc

    @pl.when(behind > 0)
    def _():
        pl.semaphore_wait(barrier, behind)

    for line in range(3):
        size, me, sem = lines[line]
        for p in range(size - 1):
            @pl.when(p < me)
            def _():
                pl.semaphore_signal(sem, inc=1, device_id=device[line](p), device_id_type=MESH)

    def answered(line):
        size, me, sem = lines[line]

        @pl.when(me < size - 1)
        def _():
            pl.semaphore_wait(sem, size - 1 - me)

    def make(src, dst, ss, rs, dev, here):
        if here:
            return pltpu.make_async_copy(src, dst, rs)
        return pltpu.make_async_remote_copy(
            src_ref=src, dst_ref=dst, send_sem=ss, recv_sem=rs, device_id=dev, device_id_type=MESH)

    def wait_for(ref, sem):
        pltpu.make_async_copy(ref, ref, sem).wait()

    def copy_y(p, here):
        piece = kvin.at[:, :, pl.ds(pl.multiple_of(p * (2 * D), 2 * D), 2 * D)]
        return make(piece, kvy.at[:, y], sy, ry.at[y], device[0](p), here)

    extra = (zl == 1) & (zh >= 2)
    index = zl * 4 + zh
    first_row = jnp.where(zh >= 2, 0, zh + 1)

    def send_z(kv, k, h, group):
        row, head = rem(first_row + k, 4), zl if h == 0 else 1 - zl
        sent = row >= group
        if group == 2:
            sent = sent & extra

        def copy(here):
            piece = kvy.at[kv, row - group, :, pl.ds(pl.multiple_of(head * D, D), D)]
            slot = 10 - 8 * group + index if group < 2 else zh - 2
            return make(piece, both[kv].at[slot], sz.at[group], rz.at[kv, group],
                        (y * 2 + head, row * 8 + xc), here)

        if h:
            @pl.when(sent)
            def _():
                copy(False).start()
        else:
            @pl.when(sent & (row != zh))
            def _():
                copy(False).start()

            @pl.when(sent & (row == zh))
            def _():
                copy(True).start()

    def place_x(i):
        return rem(x + i // 2, 4), core if i % 2 == 0 else 1 - core

    def send_x(kv, i, which):
        xd, cd = place_x(i)
        s0 = 10 + 2 * xd + cd
        src, dst, rs = (
            (both[kv].at[s0], own.at[kv, 1 + e, qr], rx.at[kv, 0]),
            (both[kv].at[s0 - 1], own.at[kv, 0, qr], rx.at[kv, 0]),
            (st.at[kv, i], pre.at[kv, :, e, qr], rx.at[kv, 1]),
        )[which]
        make(src, dst, sx.at[which], rs, (c, zh * 8 + xd * 2 + cd), i == 0).start()

    wait_for(kvin, in_sem)
    for p in range(3):
        @pl.when(p < y)
        def _():
            copy_y(p, False).start()

    copy_y(y, True).start()
    answered(0)
    for p in range(1, 4):
        @pl.when(p > y)
        def _():
            copy_y(p, False).start()

    for kv in range(2):
        for k in range(4):
            if kv == 0:
                wait_for(kvy.at[:, 0], ry.at[rem(first_row + k, 4)])
                if k == 0:
                    answered(1)
            for h in range(2):
                send_z(kv, k, h, 0)
        for k in range(4):
            for h in range(2):
                send_z(kv, k, h, 1)
                send_z(kv, k, h, 2)

    answered(2)
    bounds_copy.wait()
    for kv in range(2):
        wait_for(both[kv].at[10:18], rz.at[kv, 0])

        @pl.when(zh >= 1)
        def _():
            wait_for(both[kv].at[2:10], rz.at[kv, 1])

        @pl.when(zh >= 2)
        def _():
            wait_for(both[kv].at[0:2], rz.at[kv, 2])

        for i in range(8):
            xd, cd = place_x(i)
            p = bounds[1, 16 * zh + 4 * xd + 2 * cd] - 16 * zh + 20
            first = jnp.clip(lax.shift_right_arithmetic(p - e + 1, 1), 0, 16)
            for w in range(2):
                st[kv, i, w] = both[kv][first + rem(first + w, 2)]
        for i in range(7, -1, -1):
            send_x(kv, i, 0)

        @pl.when(e == 1)
        def _():
            for i in range(7, -1, -1):
                send_x(kv, i, 1)

        for i in range(7, -1, -1):
            send_x(kv, i, 2)

    def arrived_x(kv):
        wait_for(own.at[kv], rx.at[kv, 0])
        wait_for(pre.at[kv], rx.at[kv, 1])

    b0 = 16 * zh + 4 * x + 2 * core
    p0 = bounds[1, b0]
    rows_i = lax.broadcasted_iota(jnp.int32, (2 * BLK, BLK), 0) % BLK
    cols_i = lax.broadcasted_iota(jnp.int32, (2 * BLK, BLK), 1)
    causal = cols_i <= rows_i
    q_copy.wait()
    arrived_x(0)
    kp = pre[0].reshape(4 * BLK, D)
    for i in range(2):
        b = b0 + i
        own0, lo, hi1 = bounds[0, b], bounds[1, b], bounds[2, b]
        response = lo < hi1
        hi = jnp.where(response, hi1, b)
        keep = []
        for u in range(4):
            block = p0 + (u + 64 - p0) % 4
            keep.append((lo <= block) & (block < hi))
        keep.append(response & (own0 < b))
        kc = jnp.concatenate([kp, own[0, i:i + 2].reshape(2 * BLK, D)], axis=0)
        for g in range(0, G, 2):
            q2 = jnp.concatenate(
                [q_v[i * BLK:(i + 1) * BLK, (g + h) * D:(g + h + 1) * D] for h in range(2)], axis=0)
            s = lax.dot_general(q2, kc, (((1,), (1,)), ((), ())),
                                preferred_element_type=jnp.float32) * SCALE
            tiles = []
            for u in range(6):
                tile = s[:, u * BLK:(u + 1) * BLK]
                tiles.append(jnp.where(keep[u] if u < 5 else causal, tile, NEG))
            top = tiles[0]
            for tile in tiles[1:]:
                top = jnp.maximum(top, tile)
            top = jnp.max(top, axis=1, keepdims=True)
            for u in range(6):
                w_v[i * 4 + g // 2, :, u * BLK:(u + 1) * BLK] = jnp.exp2(tiles[u] - top).astype(jnp.bfloat16)

    arrived_x(1)
    vp = pre[1].reshape(4 * BLK, D)
    ones = jnp.ones((6 * BLK, D), jnp.bfloat16)

    for i in range(2):
        vc = jnp.concatenate([vp, own[1, i:i + 2].reshape(2 * BLK, D)], axis=0)
        vc = jnp.concatenate([vc, ones], axis=1)
        for g in range(0, G, 2):
            o = jnp.dot(w_v[i * 4 + g // 2], vc, preferred_element_type=jnp.float32)
            o = (o[:, :D] / o[:, D:]).astype(jnp.bfloat16)
            for h in range(2):
                out_ref[i * BLK:(i + 1) * BLK, (g + h) * D:(g + h + 1) * D] = o[h * BLK:(h + 1) * BLK]

    wait_for(kvy.at[:, 0:3], sy)
    wait_for(st.at[0, 0:7], sz.at[0])

    @pl.when(zh == 0)
    def _():
        wait_for(st.at[0, 0:6], sz.at[1])

    @pl.when(zh >= 1)
    def _():
        wait_for(st.at[0, 0:5], sz.at[1])

    @pl.when(extra)
    def _():
        wait_for(st.at[0, 0:3], sz.at[2])

    wait_for(st.at[0, 0:7], sx.at[0])

    @pl.when(e == 1)
    def _():
        wait_for(st.at[0, 0:7], sx.at[1])

    wait_for(st.at[:, 0:7], sx.at[2])


def local(queries, keys, values, bounds):
    dma = pltpu.SemaphoreType.DMA
    vmem = lambda *shape: pltpu.VMEM(shape, jnp.bfloat16)
    return pl.pallas_call(
        kernel,
        out_shape=jax.ShapeDtypeStruct((256, G * D), jnp.bfloat16),
        in_specs=[pl.BlockSpec(memory_space=pltpu.HBM)] * 4,
        out_specs=pl.BlockSpec(memory_space=pltpu.VMEM),
        scratch_shapes=[
            pltpu.SMEM((3, 64), jnp.int32), vmem(256, G * D), vmem(2, QT, G * D), vmem(2, 4, QT, 2 * D), vmem(18, QT, D), vmem(18, QT, D),
            vmem(2, 8, 2, QT, D), vmem(2, 2, 2, 4, QT, D), vmem(2, 3, 4, QT, D),
            vmem(8, 2 * BLK, 6 * BLK),
            *[pltpu.SemaphoreType.REGULAR] * 3,
            dma, dma, dma, dma, dma((3,)), dma((3,)), dma((4,)), dma((2, 3)), dma((2, 2)),
        ],
        compiler_params=pltpu.CompilerParams(collective_id=0, has_side_effects=True,
                                             vmem_limit_bytes=50 * 2 ** 20),
        cost_estimate=pl.CostEstimate(flops=8 * 10 ** 8, bytes_accessed=2 ** 21,
                                      transcendentals=1536 * 1024),
    )(*[pltpu.with_memory_space_constraint(a, pltpu.HBM) for a in (bounds, queries, keys, values)])


def solution(mesh):
    in_specs = (P("ctx", None), P(("cuts", "ctx"), None), P(("cuts", "ctx"), None), P())
    return jax.shard_map(local, mesh=mesh, in_specs=in_specs, out_specs=P("ctx", "cuts"),
                         check_vma=False)
```

```python
import jax
import jax.numpy as jnp
from jax import lax
from jax.experimental import pallas as pl
from jax.experimental.pallas import tpu as pltpu
from jax.sharding import PartitionSpec as P

D = 128
QT = 32
G = 8
BLK = 128
NEG = -1e30
MESH = pl.DeviceIdType.MESH
SCALE = 128 ** -0.5 * 1.4426950408889634


def rem(a, b):
    return lax.rem(a, jnp.int32(b))


def kernel(bounds_hbm, q_hbm, k_hbm, v_hbm, out_ref,
           bounds, q_v, kvin, kvy, kbuf, vbuf, st, pre, own, w_v,
           gy, gz, gx, bounds_sem, q_sem, in_sem, sy, sz, sx, ry, rz, rx):
    c = lax.axis_index("cuts")
    t = lax.axis_index("ctx")
    y, zl = lax.div(c, jnp.int32(2)), rem(c, 2)
    zh, xc = lax.div(t, jnp.int32(8)), rem(t, 8)
    x, core = lax.div(xc, jnp.int32(2)), rem(xc, 2)
    e = lax.div(x, jnp.int32(2))
    qr = rem(x, 2) * 2 + core
    z = zh * 2 + zl

    both = (kbuf, vbuf)
    k_copy = pltpu.make_async_copy(k_hbm, kvin.at[0], in_sem)
    v_copy = pltpu.make_async_copy(v_hbm, kvin.at[1], in_sem)
    q_copy = pltpu.make_async_copy(
        q_hbm.at[:, pl.ds(pl.multiple_of(c * (G * D), G * D), G * D)], q_v, q_sem)
    k_copy.start()
    v_copy.start()
    bounds_copy = pltpu.make_async_copy(bounds_hbm, bounds, bounds_sem)
    bounds_copy.start()

    device = (
        lambda p: (p * 2 + zl, t),
        lambda p: (y * 2 + rem(p, 2), lax.div(p, jnp.int32(2)) * 8 + xc),
        lambda p: (c, zh * 8 + p),
    )
    lines = ((4, y, gy), (8, z, gz), (8, xc, gx))

    @pl.when(zh <= 1)
    def _():
        kbuf[0:10] = jnp.zeros((10, QT, D), jnp.bfloat16)
        vbuf[0:10] = jnp.zeros((10, QT, D), jnp.bfloat16)

    barrier = pltpu.get_barrier_semaphore()
    for line in range(3):
        size, me, _ = lines[line]

        def greet(p, carry):
            pl.semaphore_signal(barrier, inc=1, device_id=device[line](p), device_id_type=MESH)
            return carry

        lax.fori_loop(me + 1, size, greet, 0)

    q_copy.start()
    behind = y + z + xc

    @pl.when(behind > 0)
    def _():
        pl.semaphore_wait(barrier, behind)

    for line in range(3):
        size, me, sem = lines[line]

        def answer(p, carry):
            pl.semaphore_signal(sem.at[zh] if line == 1 else sem, inc=1, device_id=device[line](p),
                                device_id_type=MESH)
            return carry

        lax.fori_loop(0, me, answer, 0)

    def answered(line):
        size, me, sem = lines[line]

        @pl.when(me < size - 1)
        def _():
            pl.semaphore_wait(sem, size - 1 - me)

    def row_ready(row):
        later = jnp.clip(2 * row + 1 - z, 0, 2)

        @pl.when(later > 0)
        def _():
            pl.semaphore_wait(gz.at[row], later)

    def make(src, dst, ss, rs, dev, here):
        if here:
            return pltpu.make_async_copy(src, dst, rs)
        return pltpu.make_async_remote_copy(
            src_ref=src, dst_ref=dst, send_sem=ss, recv_sem=rs, device_id=dev, device_id_type=MESH)

    def wait_for(ref, sem):
        pltpu.make_async_copy(ref, ref, sem).wait()

    def copy_y(p, here):
        piece = kvin.at[:, :, pl.ds(pl.multiple_of(p * (2 * D), 2 * D), 2 * D)]
        return make(piece, kvy.at[:, y], sy, ry.at[y], device[0](p), here)

    extra = (zl == 1) & (zh >= 2)
    index = zl * 4 + zh
    turn = (zh == 2).astype(jnp.int32)

    def place_z(k):
        return zh if k == 3 else rem(zh + 1 + turn * ((k + 1) % 3) + (1 - turn) * k, 4)

    def send_z(kv, k, h, group):
        row, head = place_z(k), zl if h == 0 else 1 - zl
        piece = kvy.at[kv, row - group, :, pl.ds(pl.multiple_of(head * D, D), D)]
        slot = 10 - 8 * group + index if group < 2 else zh - 2

        def start():
            make(piece, both[kv].at[slot], sz.at[group], rz.at[kv, group],
                 (y * 2 + head, row * 8 + xc), k == 3 and h == 0).start()

        if group == 0:
            start()
        else:
            pl.when(row >= group)(start)

    def place_x(i):
        return rem(x + i // 2, 4), core if i % 2 == 0 else 1 - core

    def send_x(kv, i, which):
        xd, cd = place_x(i)
        s0 = 10 + 2 * xd + cd
        src, dst, rs = (
            (both[kv].at[s0], own.at[kv, 1 + e, qr], rx.at[kv, 0]),
            (both[kv].at[s0 - 1], own.at[kv, 0, qr], rx.at[kv, 0]),
            (st.at[kv, i], pre.at[kv, :, e, qr], rx.at[kv, 1]),
        )[which]
        make(src, dst, sx.at[which], rs, (c, zh * 8 + xd * 2 + cd), i == 0).start()

    wait_for(kvin, in_sem)
    for p in range(3):
        @pl.when(p < y)
        def _():
            copy_y(p, False).start()

    copy_y(y, True).start()
    answered(0)
    for p in range(1, 4):
        @pl.when(p > y)
        def _():
            copy_y(p, False).start()

    @pl.when(zh <= 1)
    def _():
        for yp in range(4):
            wait_for(kvy.at[:, 0], ry.at[yp])

    for k in range(4):
        for yp in ((0,), (1,), (2, 3), ())[k]:
            @pl.when(zh >= 2)
            def _():
                wait_for(kvy.at[:, 0], ry.at[yp])

        row_ready(place_z(k))
        for kv in range(2):
            for h in range(2):
                send_z(kv, k, h, 0)
            for h in range(2):
                send_z(kv, k, h, 1)

        @pl.when(extra)
        def _():
            for kv in range(2):
                for h in range(2):
                    send_z(kv, k, h, 2)

    answered(2)
    bounds_copy.wait()
    for kv in range(2):
        wait_for(both[kv].at[10:18], rz.at[kv, 0])
        for i in range(7, -1, -1):
            send_x(kv, i, 0)

        @pl.when(zh >= 1)
        def _():
            wait_for(both[kv].at[2:10], rz.at[kv, 1])

        @pl.when(zh >= 2)
        def _():
            wait_for(both[kv].at[0:2], rz.at[kv, 2])

        for i in range(8):
            xd, cd = place_x(i)
            p = bounds[1, 16 * zh + 4 * xd + 2 * cd] - 16 * zh + 20
            first = jnp.clip(lax.shift_right_arithmetic(p - e + 1, 1), 0, 16)
            for w in range(2):
                st[kv, i, w] = both[kv][first + rem(first + w, 2)]
        @pl.when(e == 1)
        def _():
            for i in range(7, -1, -1):
                send_x(kv, i, 1)

        for i in range(7, -1, -1):
            send_x(kv, i, 2)

    def arrived_x(kv):
        wait_for(own.at[kv], rx.at[kv, 0])
        wait_for(pre.at[kv], rx.at[kv, 1])

    b0 = 16 * zh + 4 * x + 2 * core
    p0 = bounds[1, b0]
    rows_i = lax.broadcasted_iota(jnp.int32, (2 * BLK, BLK), 0) % BLK
    cols_i = lax.broadcasted_iota(jnp.int32, (2 * BLK, BLK), 1)
    causal = cols_i <= rows_i
    q_copy.wait()
    arrived_x(0)
    kp = pre[0].reshape(4 * BLK, D)
    for i in range(2):
        b = b0 + i
        own0, lo, hi1 = bounds[0, b], bounds[1, b], bounds[2, b]
        response = lo < hi1
        hi = jnp.where(response, hi1, b)
        keep = []
        for u in range(4):
            block = p0 + (u + 64 - p0) % 4
            keep.append((lo <= block) & (block < hi))
        keep.append(response & (own0 < b))
        kc = jnp.concatenate([kp, own[0, i:i + 2].reshape(2 * BLK, D)], axis=0)
        for g in range(0, G, 2):
            q2 = jnp.concatenate(
                [q_v[i * BLK:(i + 1) * BLK, (g + h) * D:(g + h + 1) * D] for h in range(2)], axis=0)
            s = lax.dot_general(q2, kc, (((1,), (1,)), ((), ())),
                                preferred_element_type=jnp.float32) * SCALE
            tiles = []
            for u in range(6):
                tile = s[:, u * BLK:(u + 1) * BLK]
                tiles.append(jnp.where(keep[u] if u < 5 else causal, tile, NEG))
            top = tiles[0]
            for tile in tiles[1:]:
                top = jnp.maximum(top, tile)
            top = jnp.max(top, axis=1, keepdims=True)
            for u in range(6):
                w_v[i * 4 + g // 2, :, u * BLK:(u + 1) * BLK] = jnp.exp2(tiles[u] - top).astype(jnp.bfloat16)

    arrived_x(1)
    vp = pre[1].reshape(4 * BLK, D)
    ones = jnp.ones((6 * BLK, D), jnp.bfloat16)

    for i in range(2):
        vc = jnp.concatenate([vp, own[1, i:i + 2].reshape(2 * BLK, D)], axis=0)
        vc = jnp.concatenate([vc, ones], axis=1)
        for g in range(0, G, 2):
            o = jnp.dot(w_v[i * 4 + g // 2], vc, preferred_element_type=jnp.float32)
            o = (o[:, :D] / o[:, D:]).astype(jnp.bfloat16)
            for h in range(2):
                out_ref[i * BLK:(i + 1) * BLK, (g + h) * D:(g + h + 1) * D] = o[h * BLK:(h + 1) * BLK]

    wait_for(kvy.at[:, 0:3], sy)
    wait_for(st.at[0, 0:7], sz.at[0])

    @pl.when(zh == 0)
    def _():
        wait_for(st.at[0, 0:6], sz.at[1])

    @pl.when(zh >= 1)
    def _():
        wait_for(st.at[0, 0:5], sz.at[1])

    @pl.when(extra)
    def _():
        wait_for(st.at[0, 0:3], sz.at[2])

    wait_for(st.at[0, 0:7], sx.at[0])

    @pl.when(e == 1)
    def _():
        wait_for(st.at[0, 0:7], sx.at[1])

    wait_for(st.at[:, 0:7], sx.at[2])


def local(queries, keys, values, bounds):
    dma = pltpu.SemaphoreType.DMA
    vmem = lambda *shape: pltpu.VMEM(shape, jnp.bfloat16)
    return pl.pallas_call(
        kernel,
        out_shape=jax.ShapeDtypeStruct((256, G * D), jnp.bfloat16),
        in_specs=[pl.BlockSpec(memory_space=pltpu.HBM)] * 4,
        out_specs=pl.BlockSpec(memory_space=pltpu.VMEM),
        scratch_shapes=[
            pltpu.SMEM((3, 64), jnp.int32), vmem(256, G * D), vmem(2, QT, G * D), vmem(2, 4, QT, 2 * D), vmem(18, QT, D), vmem(18, QT, D),
            vmem(2, 8, 2, QT, D), vmem(2, 2, 2, 4, QT, D), vmem(2, 3, 4, QT, D),
            vmem(8, 2 * BLK, 6 * BLK),
            pltpu.SemaphoreType.REGULAR, pltpu.SemaphoreType.REGULAR((4,)), pltpu.SemaphoreType.REGULAR,
            dma, dma, dma, dma, dma((3,)), dma((3,)), dma((4,)), dma((2, 3)), dma((2, 2)),
        ],
        compiler_params=pltpu.CompilerParams(collective_id=0, has_side_effects=True,
                                             vmem_limit_bytes=50 * 2 ** 20),
        cost_estimate=pl.CostEstimate(flops=8 * 10 ** 8, bytes_accessed=2 ** 21,
                                      transcendentals=1536 * 1024),
    )(*[pltpu.with_memory_space_constraint(a, pltpu.HBM) for a in (bounds, queries, keys, values)])


def solution(mesh):
    in_specs = (P("ctx", None), P(("cuts", "ctx"), None), P(("cuts", "ctx"), None), P())
    return jax.shard_map(local, mesh=mesh, in_specs=in_specs, out_specs=P("ctx", "cuts"),
                         check_vma=False)
```
